128 devices in a mesh: wide: 32 (over x_hi, y, z), narrow: 4 (over x_lo, core).
Axes of the slice: x: 4 (x_hi: 2, x_lo: 2; x = x_hi * 2 + x_lo), y: 4, z: 4, core: 2. Of those that a mesh axis runs over, the one named last changes fastest.
Arguments:
- jacobian: bfloat16 [32768, 32768], P('wide', 'narrow'), may hold values from -0.03125 to 0.03125
- prior_scale: float32 [32768], P('narrow'), may hold values from 0.5 to 2
- lag_one: float32 [64], replicated, may hold values from 0.2 to 0.8
- lag_two: float32 [64], replicated, may hold values from -0.4 to 0.15
- noise_scale: float32 [64], replicated, may hold values from 0.3 to 3
- sketch_seed: int32 [1], replicated, may hold values from 0 to 1048575
Outputs:
- pulled_back: float32 [512, 32768], P('wide', 'narrow')
The draws below stay inside these ranges and needn't reach their ends.
All inputs are finite; a program needn't handle non-finite values.
Results may differ from the reference program's by a relative error of at most 0.0038.
Values may be sent and summed in bfloat16 or wider, within the bound.
A program may use at most 128 MiB of HBM per device.

```python
import math
import jax
import jax.numpy as jnp

P_SIZE = 32768
K = 512
S = 64
NT = 512
ROWS = 32768


def steps_of(own_key, shape, cuts, least, largest):
    loudness = 1.0
    for axis_at, shards_of in cuts:
        heights = jax.random.uniform(jax.random.fold_in(jax.random.fold_in(own_key, 6), axis_at), (shards_of,), jnp.float32, least / len(cuts), largest / len(cuts))
        loudness = loudness * jnp.repeat(jnp.exp(heights), shape[axis_at] // shards_of).reshape((-1,) + (1,) * (len(shape) - 1 - axis_at))
    return loudness


def scatter_about(rng, shape, scale, limit, shards=(), kind=jnp.bfloat16):
    values = jax.random.normal(rng, shape, jnp.float32) * scale
    if len(shards) > 0:
        values = steps_of(rng, shape, shards, -0.22, 0.18) * values
    return jnp.clip(values, min=-limit, max=limit).astype(kind)


def setup_inputs(seed: int = 0) -> dict:
    arg_keys = jax.random.split(jax.random.key(seed), 7)
    jacobian = scatter_about(arg_keys[0], (ROWS, P_SIZE), P_SIZE ** -0.5, 0.03125, ((0, 32), (1, 4)))
    prior_scale = jnp.clip(jnp.exp(math.log(2.0) - 1.3862944 * jax.random.uniform(arg_keys[1], (P_SIZE,), jnp.float32) ** steps_of(arg_keys[1], (P_SIZE,), ((0, 4),), -0.2, 0.2)), 0.5, 2.0)
    lag_one = jnp.clip(jax.random.uniform(arg_keys[2], (S,), jnp.float32, 0.2, 0.8), 0.2, 0.8)
    lag_two = jnp.clip(jax.random.uniform(arg_keys[3], (S,), jnp.float32, -0.4, 0.15), -0.4, 0.15)
    noise_scale = jnp.clip(jnp.exp(jax.random.uniform(arg_keys[4], (S,), jnp.float32, math.log(0.3), math.log(3.0))), 0.3, 3.0)
    sketch_seed = jax.random.randint(arg_keys[5], (1,), 0, 1048576).astype(jnp.int32)
    return {"jacobian": jacobian, "prior_scale": prior_scale, "lag_one": lag_one, "lag_two": lag_two, "noise_scale": noise_scale, "sketch_seed": sketch_seed}


def sketch_table(seed_value, row_count, first_row):
    param_index = (first_row + jnp.arange(row_count, dtype=jnp.int32))[:, None]
    column_index = jnp.arange(K, dtype=jnp.int32)[None, :]
    hashed = param_index * K + column_index
    hashed = hashed ^ (seed_value[0] * 747796405)
    hashed = hashed * -1640531535
    hashed = hashed ^ ((hashed >> 15) & 131071)
    hashed = hashed * 739982445
    hashed = hashed ^ ((hashed >> 12) & 1048575)
    hashed = hashed * 695872825
    hashed = hashed ^ ((hashed >> 15) & 131071)
    uniform = ((hashed >> 8) & 16777215).astype(jnp.float32) * (1.0 / 16777216.0)
    return 1.7320508 * (2.0 * uniform - 1.0)


def whiten_forward(values, lag_one, lag_two, noise_scale):
    prev_one = jnp.pad(values, ((1, 0), (0, 0), (0, 0)))[:-1]
    prev_two = jnp.pad(values, ((2, 0), (0, 0), (0, 0)))[:-2]
    return (values - lag_one[:, None] * prev_one - lag_two[:, None] * prev_two) / noise_scale[:, None]


def whiten_adjoint(values, lag_one, lag_two, noise_scale):
    next_one = jnp.pad(values, ((0, 1), (0, 0), (0, 0)))[1:]
    next_two = jnp.pad(values, ((0, 2), (0, 0), (0, 0)))[2:]
    return (values - lag_one[:, None] * next_one - lag_two[:, None] * next_two) / noise_scale[:, None]


def reference(jacobian, prior_scale, lag_one, lag_two, noise_scale, sketch_seed):
    sketch = (prior_scale[:, None] * sketch_table(sketch_seed, P_SIZE, 0)).astype(jnp.bfloat16)
    images = jnp.dot(jacobian, sketch, preferred_element_type=jnp.float32).reshape(NT, S, K)
    whitened = whiten_forward(images, lag_one, lag_two, noise_scale)
    adjoint = whiten_adjoint(whitened, lag_one, lag_two, noise_scale).astype(jnp.bfloat16).reshape(NT * S, K)
    product = jnp.dot(adjoint.T, jacobian, preferred_element_type=jnp.float32)
    return product * prior_scale[None, :]
```

```python
import functools

import jax
import jax.numpy as jnp
import numpy as np
from jax import lax
from jax.experimental import pallas as pl
from jax.experimental.pallas import tpu as pltpu
from jax.sharding import PartitionSpec as P

K = 512
S = 64
MESH = pl.DeviceIdType.MESH
CW = 512
HW = CW // 2
GW = 1024
M1, M2, M3 = -1640531535, 739982445, 695872825
SPREAD = float(np.float32(1.7320508) * np.float32(2.0**-23))


def kernel(
    j_hbm, prior, coef, seed, out,
    jbuf, sk0, sk1, acc, rxc, rxx, img, halo, adj,
    s_buf, r1opp, r1raw, r1sum, f1, t_f32, t_b16, r2opp, r2raw, r2sum, f2, u_f32, u_b16, r3,
    j_sem, a_send, a_recv, b_send, b_recv,
):
    n_chunks = jbuf.shape[0]
    rows = jbuf.shape[1]
    width = n_chunks * CW
    wide, narrow = lax.axis_index("wide"), lax.axis_index("narrow")
    xh, y, z = wide // 16, (wide // 4) % 4, wide % 4
    xl, core = narrow // 2, narrow % 2
    at = lambda w: (w, narrow)
    mate = (wide, xl * 2 + (1 - core))
    across = (wide, (1 - xl) * 2 + core)
    later, earlier = at((wide + 1) % 32), at((wide + 31) % 32)
    rights = (at(xh * 16 + ((y + 1) % 4) * 4 + z), at(xh * 16 + y * 4 + (z + 1) % 4))
    lefts = (at(xh * 16 + ((y + 3) % 4) * 4 + z), at(xh * 16 + y * 4 + (z + 3) % 4))
    xmate = at((1 - xh) * 16 + y * 4 + z)

    def load(c):
        return pltpu.make_async_copy(
            j_hbm.at[:, pl.ds(pl.multiple_of(c * CW, CW), CW)], jbuf.at[c], j_sem.at[c]
        )

    @pl.loop(0, n_chunks)
    def _(c):
        load(c).start()

    barrier = pltpu.get_barrier_semaphore()
    partners = (mate, across, later, earlier, *rights, *lefts, xmate)
    for partner in partners:
        pl.semaphore_signal(barrier, inc=1, device_id=partner, device_id_type=MESH)

    salt = seed[0] * 747796405
    salt_high, salt_low = salt & -512, salt & 511

    def generate(g, dest):
        first = narrow * width + g * GW
        across_p = (
            ((lax.broadcasted_iota(jnp.int32, (16, GW), 1) + first) * 512) ^ salt_high
        ) * M1
        scale = jnp.broadcast_to(prior[:, pl.ds(pl.multiple_of(g * GW, GW), GW)], (16, GW))
        for block in range(K // 16):
            down = lax.broadcasted_iota(jnp.int32, (16, 128), 0) + block * 16
            down = (down ^ salt_low) * M1
            h = across_p + jnp.concatenate([down] * (GW // 128), axis=1)
            h = h ^ lax.shift_right_logical(h, 15)
            h = h * M2
            h = h ^ lax.shift_right_logical(h, 12)
            h = h * M3
            h = h ^ lax.shift_right_logical(h, 15)
            h = lax.shift_right_logical(h, 8) - 8388608
            omega = h.astype(jnp.float32) * SPREAD
            dest[block * 16 : block * 16 + 16, :] = (scale * omega).astype(jnp.bfloat16)

    def multiply(g, source):
        total = acc[...].reshape(K, rows)
        for part in range(GW // CW):
            load(g * (GW // CW) + part).wait()
            total += lax.dot_general(
                source[:, part * CW : part * CW + CW],
                jbuf[g * (GW // CW) + part],
                (((1,), (1,)), ((), ())),
                preferred_element_type=jnp.float32,
            )
        acc[...] = total.reshape(acc.shape)

    acc[...] = jnp.zeros_like(acc)
    generate(0, sk0)
    n_gen = width // GW

    @pl.loop(0, n_gen // 2)
    def _(i):
        multiply(2 * i, sk0)
        generate(2 * i + 1, sk1)
        multiply(2 * i + 1, sk1)
        generate((2 * i + 2) % n_gen, sk0)

    pl.semaphore_wait(barrier, len(partners))

    def to_mate(slot):
        x = (1 - xl) if slot == 0 else xl
        return pltpu.make_async_remote_copy(
            acc.at[x * 2 + (1 - core)], rxc.at[slot], a_send.at[slot], a_recv.at[slot],
            device_id=mate, device_id_type=MESH,
        )

    edges = ((0, 128), (rows - 128, rows), (128, rows - 128))

    def to_across(piece):
        low, high = edges[piece]
        return pltpu.make_async_remote_copy(
            rxx.at[1, :, low:high], rxx.at[0, :, low:high],
            a_send.at[2 + piece], a_recv.at[2 + piece],
            device_id=across, device_id_type=MESH,
        )

    def to_time(side):
        src = img.at[:, 128:256] if side == 0 else img.at[:, rows : rows + 128]
        return pltpu.make_async_remote_copy(
            src, halo.at[side], a_send.at[5 + side], a_recv.at[5 + side],
            device_id=earlier if side == 0 else later, device_id_type=MESH,
        )

    to_mate(0).start()
    to_mate(1).start()
    to_mate(0).wait_recv()
    rxx[1] = acc[(1 - xl) * 2 + core] + rxc[0]
    for piece in range(3):
        to_across(piece).start()
    to_mate(1).wait_recv()
    rxc[1] = acc[xl * 2 + core] + rxc[1]
    for piece in range(3):
        low, high = edges[piece]
        to_across(piece).wait_recv()
        img[:, 128 + low : 128 + high] = rxc[1, :, low:high] + rxx[0, :, low:high]
        if piece < 2:
            to_time(piece).start()
    to_time(0).wait_recv()
    to_time(1).wait_recv()
    to_time(0).wait_send()
    to_time(1).wait_send()
    img[:, rows + 128 :] = halo[0]
    img[:, :128] = jnp.where(wide == 0, jnp.zeros((128, 128), jnp.float32), halo[1])

    whole = rows + 256
    reps = whole // 128
    spread = lambda i: jnp.concatenate([jnp.broadcast_to(coef[i : i + 1, :], (32, 128))] * reps, axis=1)
    lag_one, lag_two, scale = spread(0), spread(1), spread(2)
    lane = lax.broadcasted_iota(jnp.int32, (32, whole), 1)
    limit = jnp.where(wide == 31, rows + 128, whole)
    mine = xl * 2 + core
    for block in range(4):
        part = slice(block * 32, block * 32 + 32)
        v = img[part, :]
        w = (v - lag_one * pltpu.roll(v, S, 1) - lag_two * pltpu.roll(v, 2 * S, 1)) / scale
        w = jnp.where(lane < limit, w, 0.0)
        a = (
            w - lag_one * pltpu.roll(w, whole - S, 1) - lag_two * pltpu.roll(w, whole - 2 * S, 1)
        ) / scale
        adj[mine, part, :] = a[:, 128 : 128 + rows].astype(jnp.bfloat16)

    def share(which):
        q = mine if which < 2 else (1 - xl) * 2 + core
        return pltpu.make_async_remote_copy(
            adj.at[q], adj.at[q], a_send.at[7 + which], a_recv.at[7 + which],
            device_id=across if which == 0 else mate, device_id_type=MESH,
        )

    share(0).start()
    share(1).start()
    share(0).wait_recv()
    share(2).start()
    share(1).wait_recv()
    share(2).wait_recv()

    def remote(c, kind, src, dst, device):
        return pltpu.make_async_remote_copy(
            src, dst, b_send.at[c, kind], b_recv.at[c, kind],
            device_id=device, device_id_type=MESH,
        )

    def place(color):
        return (y, z) if color == 0 else (z, y)

    def own(color, c, h, j):
        return s_buf.at[c, h, :, j] if color == 0 else s_buf.at[c, h, :, :, j]

    def first(color, c, kind):
        d = place(color)[0]
        right, left = rights[color], lefts[color]
        if kind == 0:
            return remote(c, 0, own(color, c, 0, (d + 2) % 4), r1opp.at[c, 0], right)
        if kind == 1:
            return remote(c, 1, own(color, c, 1, (d + 2) % 4), r1opp.at[c, 1], left)
        if kind == 2:
            return remote(c, 2, own(color, c, 1, (d + 1) % 4), r1raw.at[c, 0], right)
        if kind == 3:
            return remote(c, 3, own(color, c, 0, (d + 3) % 4), r1raw.at[c, 1], left)
        if kind == 4:
            return remote(c, 4, f1.at[c, 0], r1sum.at[c, 0], right)
        return remote(c, 5, f1.at[c, 1], r1sum.at[c, 1], left)

    def second(color, c, kind):
        d = place(color)[1]
        right, left = rights[1 - color], lefts[1 - color]
        if kind == 0:
            return remote(c, 6, t_b16.at[c, 0, :, (d + 2) % 4], r2opp.at[c, 0], right)
        if kind == 1:
            return remote(c, 7, t_b16.at[c, 1, :, (d + 2) % 4], r2opp.at[c, 1], left)
        if kind == 2:
            return remote(c, 8, t_b16.at[c, 1, :, (d + 1) % 4], r2raw.at[c, 0], right)
        if kind == 3:
            return remote(c, 9, t_b16.at[c, 0, :, (d + 3) % 4], r2raw.at[c, 1], left)
        if kind == 4:
            return remote(c, 10, f2.at[c, 0], r2sum.at[c, 0], right)
        return remote(c, 11, f2.at[c, 1], r2sum.at[c, 1], left)

    def third(c):
        return remote(c, 12, u_b16.at[c, 1 - xh], r3.at[c], xmate)

    f32 = lambda v: v.astype(jnp.float32)

    def product(color, c):
        lhs = adj[...].reshape(K, rows)
        for h in range(2):
            value = jnp.dot(
                lhs, jbuf[c, :, h * HW : h * HW + HW], preferred_element_type=jnp.float32
            )
            s_buf[c, h] = value.astype(jnp.bfloat16).reshape(s_buf.shape[2:])
        for kind in range(4):
            first(color, c, kind).start()

    def relay_one(color, c):
        d = place(color)[0]
        for side in range(2):
            first(color, c, side).wait_recv()
            mine_ref = own(color, c, side, (d + (1 if side == 0 else 3)) % 4)
            f1[c, side] = (f32(r1opp[c, side]) + f32(mine_ref[...])).astype(jnp.bfloat16)
            first(color, c, 4 + side).start()

    def finish_one(color, c):
        d = place(color)[0]
        for kind in range(2, 6):
            first(color, c, kind).wait_recv()
        for h in range(2):
            value = f32(own(color, c, h, d)[...]) + f32(r1sum[c, h]) + f32(r1raw[c, 1 - h])
            t_f32[c, h] = value
            t_b16[c, h] = value.astype(jnp.bfloat16)
        for kind in range(4):
            second(color, c, kind).start()

    def relay_two(color, c):
        d = place(color)[1]
        for side in range(2):
            second(color, c, side).wait_recv()
            value = f32(r2opp[c, side]) + t_f32[c, side, :, (d + (1 if side == 0 else 3)) % 4]
            f2[c, side] = value.astype(jnp.bfloat16)
            second(color, c, 4 + side).start()

    def finish_two(color, c):
        d = place(color)[1]
        for kind in range(2, 6):
            second(color, c, kind).wait_recv()
        for h in range(2):
            value = t_f32[c, h, :, d] + f32(r2sum[c, h]) + f32(r2raw[c, 1 - h])
            for x in range(2):
                u_f32[c, x, h] = value[x]
                u_b16[c, x, h] = value[x].astype(jnp.bfloat16)
        third(c).start()

    def finish(color, c):
        third(c).wait_recv()
        for h in range(2):
            lanes = pl.ds(pl.multiple_of(c * CW + h * HW, HW), HW)
            out[:, lanes] = u_f32[c, xh, h] + f32(r3[c, h])

    stages = (product, relay_one, finish_one, relay_two, finish_two, finish)
    n_rounds = n_chunks // 2

    @pl.loop(0, n_rounds + len(stages) - 1)
    def _(i):
        for lag, stage in enumerate(stages):

            @pl.when((i >= lag) & (i < n_rounds + lag))
            def _():
                for color in range(2):
                    stage(color, 2 * (i - lag) + color)

    to_mate(0).wait_send()
    to_mate(1).wait_send()
    for piece in range(3):
        to_across(piece).wait_send()
    for which in range(3):
        share(which).wait_send()

    @pl.loop(0, n_rounds)
    def _(i):
        for color in range(2):
            c = 2 * i + color
            for kind in range(6):
                first(color, c, kind).wait_send()
                second(color, c, kind).wait_send()
            third(c).wait_send()


def shards(jacobian, prior_scale, lag_one, lag_two, noise_scale, sketch_seed):
    rows, width = jacobian.shape
    n = width // CW
    coef = jnp.stack([lag_one, lag_two, noise_scale])
    coef = jnp.concatenate([coef, coef], axis=1)
    bf16, f32 = jnp.bfloat16, jnp.float32
    vmem = pl.BlockSpec(memory_space=pltpu.VMEM)
    product = pl.pallas_call(
        kernel,
        out_shape=jax.ShapeDtypeStruct((K // 32, width), f32),
        in_specs=[
            pl.BlockSpec(memory_space=pl.ANY), vmem, vmem, pl.BlockSpec(memory_space=pltpu.SMEM),
        ],
        out_specs=vmem,
        scratch_shapes=[
            pltpu.VMEM((n, rows, CW), bf16),
            pltpu.VMEM((K, GW), bf16),
            pltpu.VMEM((K, GW), bf16),
            pltpu.VMEM((4, K // 4, rows), f32),
            pltpu.VMEM((2, K // 4, rows), f32),
            pltpu.VMEM((2, K // 4, rows), f32),
            pltpu.VMEM((K // 4, rows + 256), f32),
            pltpu.VMEM((2, K // 4, 128), f32),
            pltpu.VMEM((4, K // 4, rows), bf16),
            pltpu.VMEM((n, 2, 2, 4, 4, 16, HW), bf16),
            pltpu.VMEM((n, 2, 2, 4, 16, HW), bf16),
            pltpu.VMEM((n, 2, 2, 4, 16, HW), bf16),
            pltpu.VMEM((n, 2, 2, 4, 16, HW), bf16),
            pltpu.VMEM((n, 2, 2, 4, 16, HW), bf16),
            pltpu.VMEM((n, 2, 2, 4, 16, HW), f32),
            pltpu.VMEM((n, 2, 2, 4, 16, HW), bf16),
            pltpu.VMEM((n, 2, 2, 16, HW), bf16),
            pltpu.VMEM((n, 2, 2, 16, HW), bf16),
            pltpu.VMEM((n, 2, 2, 16, HW), bf16),
            pltpu.VMEM((n, 2, 2, 16, HW), bf16),
            pltpu.VMEM((n, 2, 2, 16, HW), f32),
            pltpu.VMEM((n, 2, 2, 16, HW), bf16),
            pltpu.VMEM((n, 2, 16, HW), bf16),
            pltpu.SemaphoreType.DMA((n,)),
            pltpu.SemaphoreType.DMA((10,)),
            pltpu.SemaphoreType.DMA((10,)),
            pltpu.SemaphoreType.DMA((n, 13)),
            pltpu.SemaphoreType.DMA((n, 13)),
        ],
        compiler_params=pltpu.CompilerParams(
            collective_id=0, has_side_effects=True, vmem_limit_bytes=63 * 1024 * 1024
        ),
    )(jacobian, prior_scale.reshape(1, width), coef, sketch_seed)
    return product * prior_scale[None, :]


def solution(mesh):
    in_specs = (P("wide", "narrow"), P("narrow"), P(), P(), P(), P())
    out_specs = P("wide", "narrow")
    return jax.shard_map(shards, mesh=mesh, in_specs=in_specs, out_specs=out_specs, check_vma=False)
```

```python
import functools

import jax
import jax.numpy as jnp
import numpy as np
from jax import lax
from jax.experimental import pallas as pl
from jax.experimental.pallas import tpu as pltpu
from jax.sharding import PartitionSpec as P

K = 512
S = 64
MESH = pl.DeviceIdType.MESH
CW = 1024
HW = CW // 2
BLOCK = 256
KH = K // 2
Q = KH // 4
M1, M2, M3 = -1640531535, 739982445, 695872825
SPREAD = float(np.float32(1.7320508) * np.float32(2.0**-23))


def kernel(
    j_hbm, prior, lag_one_in, lag_two_in, scale_in, seed, out,
    jbuf, sk, acc, rxc, rxx, img, halo, adj,
    s_buf, r1opp, r1in, f1, t_f32, t_b16, r2opp, r2in, f2, u_f32, u_b16, r3,
    j_sem, a_send, a_recv, b_send, b_recv,
):
    rows, width = jbuf.shape
    n_chunks = width // CW
    wide, narrow = lax.axis_index("wide"), lax.axis_index("narrow")
    xh, y, z = wide // 16, (wide // 4) % 4, wide % 4
    xl, core = narrow // 2, narrow % 2
    at = lambda w: (w, narrow)
    mate = (wide, xl * 2 + (1 - core))
    across = (wide, (1 - xl) * 2 + core)
    later, earlier = at((wide + 1) % 32), at((wide + 31) % 32)
    rights = (at(xh * 16 + ((y + 1) % 4) * 4 + z), at(xh * 16 + y * 4 + (z + 1) % 4))
    lefts = (at(xh * 16 + ((y + 3) % 4) * 4 + z), at(xh * 16 + y * 4 + (z + 3) % 4))
    xmate = at((1 - xh) * 16 + y * 4 + z)

    def load(b):
        part = pl.ds(pl.multiple_of(b * BLOCK, BLOCK), BLOCK)
        return pltpu.make_async_copy(j_hbm.at[part], jbuf.at[part], j_sem.at[b])

    for b in (3, 0, 1, 2):
        load(b).start()

    barrier = pltpu.get_barrier_semaphore()
    partners = (mate, across, later, earlier, *rights, *lefts, xmate)
    for partner in partners:
        pl.semaphore_signal(barrier, inc=1, device_id=partner, device_id_type=MESH)

    salt = seed[0] * 747796405
    salt_high, salt_low = salt & -512, salt & 511

    def generate(half, g):
        first = narrow * width + g * CW
        lanes = pl.ds(pl.multiple_of(g * CW, CW), CW)
        across_p = (
            ((lax.broadcasted_iota(jnp.int32, (16, CW), 1) + first) * 512) ^ salt_high
        ) * M1
        scale = jnp.broadcast_to(prior[:, lanes] * SPREAD, (16, CW))
        for block in range(KH // 16):
            down = lax.broadcasted_iota(jnp.int32, (16, 128), 0) + (half * KH + block * 16)
            down = (down ^ salt_low) * M1
            h = across_p + jnp.concatenate([down] * (CW // 128), axis=1)
            h = h ^ lax.shift_right_logical(h, 15)
            h = h * M2
            h = h ^ lax.shift_right_logical(h, 12)
            h = h * M3
            h = h ^ lax.shift_right_logical(h, 15)
            h = lax.shift_right_logical(h, 8) - 8388608
            sk[block * 16 : block * 16 + 16, lanes] = (scale * h.astype(jnp.float32)).astype(
                jnp.bfloat16
            )

    def multiply(half, b):
        value = lax.dot_general(
            sk[...], jbuf[pl.ds(pl.multiple_of(b * BLOCK, BLOCK), BLOCK), :],
            (((1,), (1,)), ((), ())), preferred_element_type=jnp.float32,
        )
        acc[half, b] = value.reshape(acc.shape[2:])
        to_mate(half, b).start()

    def to_mate(half, b):
        return pltpu.make_async_remote_copy(
            acc.at[half, b, :, 1 - core], rxc.at[half, b],
            a_send.at[half, b], a_recv.at[half, b],
            device_id=mate, device_id_type=MESH,
        )

    def to_across(half, b):
        return pltpu.make_async_remote_copy(
            rxx.at[half, 1, b], rxx.at[half, 0, b],
            a_send.at[half, 4 + b], a_recv.at[half, 4 + b],
            device_id=across, device_id_type=MESH,
        )

    def to_time(half, side):
        low = 128 if side == 0 else rows
        return pltpu.make_async_remote_copy(
            img.at[half, :, low : low + 128], halo.at[half, side],
            a_send.at[half, 8 + side], a_recv.at[half, 8 + side],
            device_id=earlier if side == 0 else later, device_id_type=MESH,
        )

    mine = xl * 2 + core

    def share(half, which):
        q = mine if which < 2 else (1 - xl) * 2 + core
        return pltpu.make_async_remote_copy(
            adj.at[half, q], adj.at[half, q], a_send.at[half, 10 + which], a_recv.at[half, 10 + which],
            device_id=across if which == 0 else mate, device_id_type=MESH,
        )

    def sum_cores(half, b):
        to_mate(half, b).wait_recv()
        rxx[half, 1, b] = acc[half, b, 1 - xl, core] + rxc[half, b, 1 - xl]
        to_across(half, b).start()
        rxc[half, b, xl] = acc[half, b, xl, core] + rxc[half, b, xl]

    def sum_chips(half, b):
        to_across(half, b).wait_recv()
        lanes = pl.ds(pl.multiple_of(128 + b * BLOCK, 128), BLOCK)
        img[half, :, lanes] = rxc[half, b, xl] + rxx[half, 0, b]

    def send_edges(half):
        sum_chips(half, 3)

        @pl.when(wide < 31)
        def _():
            to_time(half, 1).start()

        sum_chips(half, 0)

        @pl.when(wide > 0)
        def _():
            to_time(half, 0).start()

    def whiten(half):
        sum_chips(half, 1)
        sum_chips(half, 2)

        @pl.when(wide < 31)
        def _():
            to_time(half, 0).wait_recv()
            img[half, :, rows + 128 :] = halo[half, 0]

        @pl.when(wide == 31)
        def _():
            img[half, :, rows + 128 :] = jnp.zeros((Q, 128), jnp.float32)

        @pl.when(wide > 0)
        def _():
            to_time(half, 1).wait_recv()
            img[half, :, :128] = halo[half, 1]

        @pl.when(wide == 0)
        def _():
            img[half, :, :128] = jnp.zeros((Q, 128), jnp.float32)

        whole = rows + 256
        reps = whole // 128
        spread = lambda ref: jnp.concatenate(
            [jnp.broadcast_to(jnp.concatenate([ref[...]] * 2, axis=1), (32, 128))] * reps, axis=1
        )
        lag_one, lag_two, scale = spread(lag_one_in), spread(lag_two_in), spread(scale_in)
        lane = lax.broadcasted_iota(jnp.int32, (32, whole), 1)
        limit = jnp.where(wide == 31, rows + 128, whole)
        for block in range(Q // 32):
            part = slice(block * 32, block * 32 + 32)
            v = img[half, part, :]
            w = (v - lag_one * pltpu.roll(v, S, 1) - lag_two * pltpu.roll(v, 2 * S, 1)) / scale
            w = jnp.where(lane < limit, w, 0.0)
            ahead, ahead_two = pltpu.roll(w, whole - S, 1), pltpu.roll(w, whole - 2 * S, 1)
            a = (w - lag_one * ahead - lag_two * ahead_two) / scale
            adj[half, mine, part, :] = a[:, 128 : 128 + rows].astype(jnp.bfloat16)
        share(half, 0).start()
        share(half, 1).start()

    def pass_on(half):
        share(half, 0).wait_recv()
        share(half, 2).start()

    def gather(half):
        share(half, 1).wait_recv()
        share(half, 2).wait_recv()

    @pl.loop(0, n_chunks)
    def _(g):
        generate(0, g)

    pl.semaphore_wait(barrier, len(partners))

    @pl.loop(0, 4)
    def _(i):
        b = (i + 3) % 4
        load(b).wait()
        multiply(0, b)

        @pl.when(i > 0)
        def _():
            sum_cores(0, (i + 2) % 4)

    @pl.loop(0, n_chunks)
    def _(g):
        generate(1, g)

        @pl.when(g == 1)
        def _():
            sum_cores(0, 2)

        @pl.when(g == 3)
        def _():
            send_edges(0)

        @pl.when(g == n_chunks - 1)
        def _():
            whiten(0)

    @pl.loop(0, 3)
    def _(i):
        multiply(1, (i + 3) % 4)

        @pl.when(i > 0)
        def _():
            sum_cores(1, (i + 2) % 4)

        @pl.when(i == 1)
        def _():
            pass_on(0)

    gather(0)

    def remote(u, out_sem, in_sem, src, dst, device):
        return pltpu.make_async_remote_copy(
            src, dst, b_send.at[u % 8, out_sem], b_recv.at[u, in_sem],
            device_id=device, device_id_type=MESH,
        )

    def place(color):
        return (y, z) if color == 0 else (z, y)

    def own(color, u, h, j):
        return s_buf.at[u, h, j] if color == 0 else s_buf.at[u, h, :, j]

    def first(color, u, kind):
        d = place(color)[0]
        right, left = rights[color], lefts[color]
        if kind == 0:
            return remote(u, 0, 0, own(color, u, 0, (d + 2) % 4), r1opp.at[u, 0], right)
        if kind == 1:
            return remote(u, 0, 1, own(color, u, 1, (d + 2) % 4), r1opp.at[u, 1], left)
        if kind == 2:
            return remote(u, 0, 2, own(color, u, 1, (d + 1) % 4), r1in.at[u, 0], right)
        if kind == 3:
            return remote(u, 0, 2, own(color, u, 0, (d + 3) % 4), r1in.at[u, 1], left)
        if kind == 4:
            return remote(u, 1, 2, f1.at[u, 0], r1in.at[u, 2], right)
        return remote(u, 1, 2, f1.at[u, 1], r1in.at[u, 3], left)

    def second(color, u, kind):
        d = place(color)[1]
        right, left = rights[1 - color], lefts[1 - color]
        if kind == 0:
            return remote(u, 2, 3, t_b16.at[u, 0, (d + 2) % 4], r2opp.at[u, 0], right)
        if kind == 1:
            return remote(u, 2, 4, t_b16.at[u, 1, (d + 2) % 4], r2opp.at[u, 1], left)
        if kind == 2:
            return remote(u, 2, 5, t_b16.at[u, 1, (d + 1) % 4], r2in.at[u, 0], right)
        if kind == 3:
            return remote(u, 2, 5, t_b16.at[u, 0, (d + 3) % 4], r2in.at[u, 1], left)
        if kind == 4:
            return remote(u, 3, 5, f2.at[u, 0], r2in.at[u, 2], right)
        return remote(u, 3, 5, f2.at[u, 1], r2in.at[u, 3], left)

    def third(u):
        return remote(u, 4, 6, u_b16.at[u], r3.at[u], xmate)

    def all_in(color, u, stage):
        if stage == 0:
            remote(u, 0, 2, r1in.at[u], r1in.at[u], rights[color]).wait_recv()
        else:
            remote(u, 0, 5, r2in.at[u], r2in.at[u], rights[color]).wait_recv()

    def all_out(color, u, out_sem):
        ref = (s_buf.at[u, 0], f1.at[u], t_b16.at[u, 0], f2.at[u])[out_sem]
        remote(u, out_sem, 0, ref, ref, rights[color]).wait_send()

    f32 = lambda v: v.astype(jnp.float32)
    per_half = n_chunks // 2

    def product(n, color):
        u, c = 2 * n + color, 2 * (n % per_half) + color
        lhs = adj[n // per_half].reshape(KH, rows)
        for h in range(2):
            value = jnp.dot(
                lhs, jbuf[:, pl.ds(pl.multiple_of(c * CW + h * HW, HW), HW)], preferred_element_type=jnp.float32
            )
            s_buf[u, h] = value.astype(jnp.bfloat16).reshape(s_buf.shape[2:])
        for kind in range(4):
            first(color, u, kind).start()

    def relay_one(n, color):
        u, d = 2 * n + color, place(color)[0]
        for side in range(2):
            first(color, u, side).wait_recv()
            mine_ref = own(color, u, side, (d + (1 if side == 0 else 3)) % 4)
            f1[u, side] = (f32(r1opp[u, side]) + f32(mine_ref[...])).astype(jnp.bfloat16)
            first(color, u, 4 + side).start()

    def finish_one(n, color):
        u, d = 2 * n + color, place(color)[0]
        all_in(color, u, 0)
        for h in range(2):
            value = f32(own(color, u, h, d)[...]) + f32(r1in[u, 2 + h]) + f32(r1in[u, 1 - h])
            t_f32[u, h] = value
            t_b16[u, h] = value.astype(jnp.bfloat16)
        for kind in range(4):
            second(color, u, kind).start()

    def relay_two(n, color):
        u, d = 2 * n + color, place(color)[1]
        for side in range(2):
            second(color, u, side).wait_recv()
            value = f32(r2opp[u, side]) + t_f32[u, side, (d + (1 if side == 0 else 3)) % 4]
            f2[u, side] = value.astype(jnp.bfloat16)
            second(color, u, 4 + side).start()

    def finish_two(n, color):
        u, d = 2 * n + color, place(color)[1]
        all_in(color, u, 1)
        for h in range(2):
            value = t_f32[u, h, d] + f32(r2in[u, 2 + h]) + f32(r2in[u, 1 - h])
            u_f32[u, h] = value
            u_b16[u, h] = value.astype(jnp.bfloat16)

        @pl.when(n // per_half != xh)
        def _():
            third(u).start()

    def finish(n, color):
        u, c = 2 * n + color, 2 * (n % per_half) + color

        @pl.when(n // per_half == xh)
        def _():
            third(u).wait_recv()
            for h in range(2):
                lanes = pl.ds(pl.multiple_of(c * CW + h * HW, HW), HW)
                out[:, lanes] = u_f32[u, h] + f32(r3[u, h])

    def sent_one(n, color):
        all_out(color, 2 * n + color, 0)

    def sent_two(n, color):
        all_out(color, 2 * n + color, 1)
        all_out(color, 2 * n + color, 2)

    def sent_three(n, color):
        all_out(color, 2 * n + color, 3)

        @pl.when(n // per_half != xh)
        def _():
            third(2 * n + color).wait_send()

    def sent(half):
        for b in range(4):
            to_mate(half, b).wait_send()
            to_across(half, b).wait_send()
        for which in range(3):
            share(half, which).wait_send()

        @pl.when(wide > 0)
        def _():
            to_time(half, 0).wait_send()

        @pl.when(wide < 31)
        def _():
            to_time(half, 1).wait_send()

    stages = (product, relay_one, finish_one, relay_two, finish_two, finish)
    outgoing = ((3, sent_one), (4, sent_two), (5, sent_three))
    n_rounds = 2 * per_half

    @pl.loop(0, n_rounds + len(stages) - 1)
    def _(i):
        for lag, stage in enumerate(stages):

            @pl.when((i >= lag) & (i < n_rounds + lag))
            def _():
                for color in range(2):
                    stage(i - lag, color)

            if lag == 0:

                @pl.when(i == 0)
                def _():
                    multiply(1, 2)
                    sum_cores(1, 1)

                @pl.when(i == per_half - 3)
                def _():
                    sum_cores(1, 2)
                    send_edges(1)

                @pl.when(i == per_half - 2)
                def _():
                    whiten(1)

                @pl.when(i == per_half - 1)
                def _():
                    pass_on(1)
                    gather(1)

        @pl.when((i == per_half) | (i == per_half + 1))
        def _():
            sent(i - per_half)

        for lag, stage in outgoing:

            @pl.when((i >= lag) & (i < n_rounds + lag))
            def _():
                for color in range(2):
                    stage(i - lag, color)


def shards(jacobian, prior_scale, lag_one, lag_two, noise_scale, sketch_seed):
    rows, width = jacobian.shape
    n = width // CW
    bf16, f32 = jnp.bfloat16, jnp.float32
    vmem = pl.BlockSpec(memory_space=pltpu.VMEM)
    product = pl.pallas_call(
        kernel,
        out_shape=jax.ShapeDtypeStruct((K // 32, width), f32),
        in_specs=[
            pl.BlockSpec(memory_space=pl.ANY), vmem, vmem, vmem, vmem,
            pl.BlockSpec(memory_space=pltpu.SMEM),
        ],
        out_specs=vmem,
        scratch_shapes=[
            pltpu.VMEM((rows, width), bf16),
            pltpu.VMEM((KH, width), bf16),
            pltpu.VMEM((2, 4, 2, 2, Q, BLOCK), f32),
            pltpu.VMEM((2, 4, 2, Q, BLOCK), f32),
            pltpu.VMEM((2, 2, 4, Q, BLOCK), f32),
            pltpu.VMEM((2, Q, rows + 256), f32),
            pltpu.VMEM((2, 2, Q, 128), f32),
            pltpu.VMEM((2, 4, Q, rows), bf16),
            pltpu.VMEM((2 * n, 2, 4, 4, 16, HW), bf16),
            pltpu.VMEM((2 * n, 2, 4, 16, HW), bf16),
            pltpu.VMEM((2 * n, 4, 4, 16, HW), bf16),
            pltpu.VMEM((2 * n, 2, 4, 16, HW), bf16),
            pltpu.VMEM((2 * n, 2, 4, 16, HW), f32),
            pltpu.VMEM((2 * n, 2, 4, 16, HW), bf16),
            pltpu.VMEM((2 * n, 2, 16, HW), bf16),
            pltpu.VMEM((2 * n, 4, 16, HW), bf16),
            pltpu.VMEM((2 * n, 2, 16, HW), bf16),
            pltpu.VMEM((2 * n, 2, 16, HW), f32),
            pltpu.VMEM((2 * n, 2, 16, HW), bf16),
            pltpu.VMEM((2 * n, 2, 16, HW), bf16),
            pltpu.SemaphoreType.DMA((4,)),
            pltpu.SemaphoreType.DMA((2, 13)),
            pltpu.SemaphoreType.DMA((2, 13)),
            pltpu.SemaphoreType.DMA((8, 5)),
            pltpu.SemaphoreType.DMA((2 * n, 7)),
        ],
        compiler_params=pltpu.CompilerParams(
            collective_id=0, has_side_effects=True, vmem_limit_bytes=63 * 1024 * 1024
        ),
    )(
        jacobian, prior_scale.reshape(1, width), lag_one.reshape(1, S), lag_two.reshape(1, S),
        noise_scale.reshape(1, S), sketch_seed,
    )
    return product * prior_scale[None, :]


def solution(mesh):
    in_specs = (P("wide", "narrow"), P("narrow"), P(), P(), P(), P())
    out_specs = P("wide", "narrow")
    return jax.shard_map(shards, mesh=mesh, in_specs=in_specs, out_specs=out_specs, check_vma=False)
```

```python
import functools

import jax
import jax.numpy as jnp
import numpy as np
from jax import lax
from jax.experimental import pallas as pl
from jax.experimental.pallas import tpu as pltpu
from jax.sharding import PartitionSpec as P

K = 512
S = 64
MESH = pl.DeviceIdType.MESH
GW = 1024
CW = 512
FINALS = 1
SLOTS = 8
HW = CW // 2
BLOCK = 256
KH = K // 2
Q = KH // 4
M1, M2, M3 = -1640531535, 739982445, 695872825
SPREAD = float(np.float32(1.7320508) * np.float32(2.0**-23))


def kernel(
    j_hbm, prior, lag_one_in, lag_two_in, scale_in, seed, out,
    jbuf, sk, acc, rxc, rxx, img, halo, adj,
    s_buf, r1opp, r1in, f1, t_f32, t_b16, r2opp, r2in, f2, u_f32, u_b16, r3, x_out, x_in,
    j_sem, a_send, a_recv, b_send, b_recv, x_send, x_recv,
):
    rows, width = jbuf.shape
    n_chunks = width // CW
    wide, narrow = lax.axis_index("wide"), lax.axis_index("narrow")
    xh, y, z = wide // 16, (wide // 4) % 4, wide % 4
    xl, core = narrow // 2, narrow % 2
    at = lambda w: (w, narrow)
    mate = (wide, xl * 2 + (1 - core))
    across = (wide, (1 - xl) * 2 + core)
    later, earlier = at((wide + 1) % 32), at((wide + 31) % 32)
    rights = (at(xh * 16 + ((y + 1) % 4) * 4 + z), at(xh * 16 + y * 4 + (z + 1) % 4))
    lefts = (at(xh * 16 + ((y + 3) % 4) * 4 + z), at(xh * 16 + y * 4 + (z + 3) % 4))
    xmate = at((1 - xh) * 16 + y * 4 + z)

    def load(b):
        part = pl.ds(pl.multiple_of(b * BLOCK, BLOCK), BLOCK)
        return pltpu.make_async_copy(j_hbm.at[part], jbuf.at[part], j_sem.at[b])

    for b in (3, 0, 1, 2):
        load(b).start()

    barrier = pltpu.get_barrier_semaphore()
    partners = (mate, across, later, earlier, *rights, *lefts, xmate)
    for partner in partners:
        pl.semaphore_signal(barrier, inc=1, device_id=partner, device_id_type=MESH)

    salt = seed[0] * 747796405
    salt_high, salt_low = salt & -512, salt & 511

    def generate(half, g):
        first = narrow * width + g * GW
        lanes = pl.ds(pl.multiple_of(g * GW, GW), GW)
        across_p = (
            ((lax.broadcasted_iota(jnp.int32, (16, GW), 1) + first) * 512) ^ salt_high
        ) * M1
        scale = jnp.broadcast_to(prior[:, lanes] * SPREAD, (16, GW))
        for block in range(KH // 16):
            down = lax.broadcasted_iota(jnp.int32, (16, 128), 0) + (half * KH + block * 16)
            down = (down ^ salt_low) * M1
            h = across_p + jnp.concatenate([down] * (GW // 128), axis=1)
            h = h ^ lax.shift_right_logical(h, 15)
            h = h * M2
            h = h ^ lax.shift_right_logical(h, 12)
            h = h * M3
            h = h ^ lax.shift_right_logical(h, 15)
            h = lax.shift_right_logical(h, 8) - 8388608
            sk[block * 16 : block * 16 + 16, lanes] = (scale * h.astype(jnp.float32)).astype(
                jnp.bfloat16
            )

    def multiply(half, b):
        value = lax.dot_general(
            sk[...], jbuf[pl.ds(pl.multiple_of(b * BLOCK, BLOCK), BLOCK), :],
            (((1,), (1,)), ((), ())), preferred_element_type=jnp.float32,
        )
        acc[half, b] = value.reshape(acc.shape[2:])
        to_mate(half, b).start()

    def to_mate(half, b):
        return pltpu.make_async_remote_copy(
            acc.at[half, b, :, 1 - core], rxc.at[half, b],
            a_send.at[0], a_recv.at[half, b],
            device_id=mate, device_id_type=MESH,
        )

    def to_across(half, b):
        return pltpu.make_async_remote_copy(
            rxx.at[half, 1, b], rxx.at[half, 0, b],
            a_send.at[1], a_recv.at[half, 4 + b],
            device_id=across, device_id_type=MESH,
        )

    def to_time(half, side):
        low = 128 if side == 0 else rows
        return pltpu.make_async_remote_copy(
            img.at[half, :, low : low + 128], halo.at[half, side],
            a_send.at[3 + side], a_recv.at[half, 8 + side],
            device_id=earlier if side == 0 else later, device_id_type=MESH,
        )

    mine = xl * 2 + core

    def share(half, which):
        q = mine if which < 2 else (1 - xl) * 2 + core
        return pltpu.make_async_remote_copy(
            adj.at[half, q], adj.at[half, q], a_send.at[2], a_recv.at[half, 10 + which],
            device_id=across if which == 0 else mate, device_id_type=MESH,
        )

    def sum_cores(half, b):
        to_mate(half, b).wait_recv()
        rxx[half, 1, b] = acc[half, b, 1 - xl, core] + rxc[half, b, 1 - xl]
        to_across(half, b).start()
        rxc[half, b, xl] = acc[half, b, xl, core] + rxc[half, b, xl]

    def sum_chips(half, b):
        to_across(half, b).wait_recv()
        lanes = pl.ds(pl.multiple_of(128 + b * BLOCK, 128), BLOCK)
        img[half, :, lanes] = rxc[half, b, xl] + rxx[half, 0, b]

    def send_edges(half):
        sum_chips(half, 3)

        @pl.when(wide < 31)
        def _():
            to_time(half, 1).start()

        sum_chips(half, 0)

        @pl.when(wide > 0)
        def _():
            to_time(half, 0).start()

    def whiten(half):
        sum_chips(half, 1)
        sum_chips(half, 2)

        @pl.when(wide < 31)
        def _():
            to_time(half, 0).wait_recv()
            img[half, :, rows + 128 :] = halo[half, 0]

        @pl.when(wide == 31)
        def _():
            img[half, :, rows + 128 :] = jnp.zeros((Q, 128), jnp.float32)

        @pl.when(wide > 0)
        def _():
            to_time(half, 1).wait_recv()
            img[half, :, :128] = halo[half, 1]

        @pl.when(wide == 0)
        def _():
            img[half, :, :128] = jnp.zeros((Q, 128), jnp.float32)

        whole = rows + 256
        reps = whole // 128
        spread = lambda ref: jnp.concatenate(
            [jnp.broadcast_to(jnp.concatenate([ref[...]] * 2, axis=1), (32, 128))] * reps, axis=1
        )
        lag_one, lag_two, scale = spread(lag_one_in), spread(lag_two_in), spread(scale_in)
        lane = lax.broadcasted_iota(jnp.int32, (32, whole), 1)
        limit = jnp.where(wide == 31, rows + 128, whole)
        for block in range(Q // 32):
            part = slice(block * 32, block * 32 + 32)
            v = img[half, part, :]
            w = (v - lag_one * pltpu.roll(v, S, 1) - lag_two * pltpu.roll(v, 2 * S, 1)) / scale
            w = jnp.where(lane < limit, w, 0.0)
            ahead, ahead_two = pltpu.roll(w, whole - S, 1), pltpu.roll(w, whole - 2 * S, 1)
            a = (w - lag_one * ahead - lag_two * ahead_two) / scale
            adj[half, mine, part, :] = a[:, 128 : 128 + rows].astype(jnp.bfloat16)
        share(half, 0).start()
        share(half, 1).start()

    def pass_on(half):
        share(half, 0).wait_recv()
        share(half, 2).start()

    def gather(half):
        share(half, 1).wait_recv()
        share(half, 2).wait_recv()

    @pl.loop(0, width // GW)
    def _(g):
        generate(0, g)

    pl.semaphore_wait(barrier, len(partners))

    @pl.loop(0, 4)
    def _(i):
        b = (i + 3) % 4
        load(b).wait()
        multiply(0, b)

        @pl.when(i > 0)
        def _():
            sum_cores(0, (i + 2) % 4)

    @pl.loop(0, width // GW)
    def _(g):
        generate(1, g)

        @pl.when(g == 1)
        def _():
            sum_cores(0, 2)

        @pl.when(g == 3)
        def _():
            send_edges(0)

        @pl.when(g == width // GW - 1)
        def _():
            whiten(0)

    @pl.loop(0, 3)
    def _(i):
        multiply(1, (i + 3) % 4)

        @pl.when(i > 0)
        def _():
            sum_cores(1, (i + 2) % 4)

        @pl.when(i == 1)
        def _():
            pass_on(0)

    gather(0)

    per_half = n_chunks // 2 - FINALS
    final = 2 * per_half

    def remote(u, out_sem, in_sem, src, dst, device):
        return pltpu.make_async_remote_copy(
            src, dst, b_send.at[out_sem], b_recv.at[u % (2 * SLOTS), in_sem],
            device_id=device, device_id_type=MESH,
        )

    def place(color):
        return (y, z) if color == 0 else (z, y)

    def own(color, u, h, j):
        return s_buf.at[u, h, j] if color == 0 else s_buf.at[u, h, :, j]

    def first(color, u, kind):
        d = place(color)[0]
        right, left = rights[color], lefts[color]
        if kind == 0:
            return remote(u, 0, 0, own(color, u, 0, (d + 2) % 4), r1opp.at[u, 0], right)
        if kind == 1:
            return remote(u, 0, 0, own(color, u, 1, (d + 2) % 4), r1opp.at[u, 1], left)
        if kind == 2:
            return remote(u, 0, 1, own(color, u, 1, (d + 1) % 4), r1in.at[u, 0], right)
        if kind == 3:
            return remote(u, 0, 1, own(color, u, 0, (d + 3) % 4), r1in.at[u, 1], left)
        if kind == 4:
            return remote(u, 1, 1, f1.at[u, 0], r1in.at[u, 2], right)
        return remote(u, 1, 1, f1.at[u, 1], r1in.at[u, 3], left)

    def second(color, u, kind):
        d = place(color)[1]
        right, left = rights[1 - color], lefts[1 - color]
        if kind == 0:
            return remote(u, 2, 2, t_b16.at[u, 0, (d + 2) % 4], r2opp.at[u, 0], right)
        if kind == 1:
            return remote(u, 2, 2, t_b16.at[u, 1, (d + 2) % 4], r2opp.at[u, 1], left)
        if kind == 2:
            return remote(u, 2, 3, t_b16.at[u, 1, (d + 1) % 4], r2in.at[u, 0], right)
        if kind == 3:
            return remote(u, 2, 3, t_b16.at[u, 0, (d + 3) % 4], r2in.at[u, 1], left)
        if kind == 4:
            return remote(u, 3, 3, f2.at[u, 0], r2in.at[u, 2], right)
        return remote(u, 3, 3, f2.at[u, 1], r2in.at[u, 3], left)

    def third(u):
        return pltpu.make_async_remote_copy(
            u_b16.at[u], r3.at[u], x_send.at[0], x_recv.at[0],
            device_id=xmate, device_id_type=MESH,
        )

    def all_in(color, u, in_sem):
        ref = (r1opp, r1in, r2opp, r2in)[in_sem].at[u]
        remote(u, 0, in_sem, ref, ref, rights[color]).wait_recv()

    f32 = lambda v: v.astype(jnp.float32)
    def terms(half, c, h):
        lanes = pl.ds(pl.multiple_of(c * CW + h * HW, HW), HW)
        return jnp.dot(
            adj[half].reshape(KH, rows), jbuf[:, lanes], preferred_element_type=jnp.float32
        )

    def to_x(e):
        return pltpu.make_async_remote_copy(
            x_out.at[e], x_in.at[e], x_send.at[1], x_recv.at[1 + e],
            device_id=xmate, device_id_type=MESH,
        )

    def exchange(e):
        for h in range(2):
            value = terms(1 - xh, final + e, h)
            x_out[e, h] = value.astype(jnp.bfloat16).reshape(x_out.shape[2:])
        to_x(e).start()

    def product(n, color):
        u, c = 2 * n + color, 2 * (n % per_half) + color
        for h in range(2):
            value = terms(n // per_half, c, h)
            s_buf[u, h] = value.astype(jnp.bfloat16).reshape(s_buf.shape[2:])
        for kind in range(4):
            first(color, u, kind).start()

    def product_final(n, color):
        u, e = 2 * n + color, 2 * (n - final) + color
        to_x(e).wait_recv()
        for h in range(2):
            value = terms(xh, final + e, h).reshape(s_buf.shape[2:]) + f32(x_in[e, h])
            s_buf[u, h] = value.astype(jnp.bfloat16)
        for kind in range(4):
            first(color, u, kind).start()

    def relay_one(n, color):
        u, d = 2 * n + color, place(color)[0]
        all_in(color, u, 0)
        for side in range(2):
            mine_ref = own(color, u, side, (d + (1 if side == 0 else 3)) % 4)
            f1[u, side] = (f32(r1opp[u, side]) + f32(mine_ref[...])).astype(jnp.bfloat16)
            first(color, u, 4 + side).start()

    def finish_one(n, color):
        u, d = 2 * n + color, place(color)[0]
        all_in(color, u, 1)
        for h in range(2):
            value = f32(own(color, u, h, d)[...]) + f32(r1in[u, 2 + h]) + f32(r1in[u, 1 - h])
            t_f32[u, h] = value
            t_b16[u, h] = value.astype(jnp.bfloat16)
        for kind in range(4):
            second(color, u, kind).start()

    def relay_two(n, color):
        u, d = 2 * n + color, place(color)[1]
        all_in(color, u, 2)
        for side in range(2):
            value = f32(r2opp[u, side]) + t_f32[u, side, (d + (1 if side == 0 else 3)) % 4]
            f2[u, side] = value.astype(jnp.bfloat16)
            second(color, u, 4 + side).start()

    def finish_two(n, color):
        u, d = 2 * n + color, place(color)[1]
        all_in(color, u, 3)
        for h in range(2):
            value = t_f32[u, h, d] + f32(r2in[u, 2 + h]) + f32(r2in[u, 1 - h])
            u_f32[u, h] = value
            u_b16[u, h] = value.astype(jnp.bfloat16)

        @pl.when((n < final) & (n // per_half != xh))
        def _():
            third(u).start()

        @pl.when(n >= final)
        def _():
            c = final + 2 * (n - final) + color
            for h in range(2):
                out[:, pl.ds(pl.multiple_of(c * CW + h * HW, HW), HW)] = u_f32[u, h]

    def collect():
        ref = r3.at[pl.ds(xh * final, final)]
        pltpu.make_async_remote_copy(
            ref, ref, x_send.at[0], x_recv.at[0], device_id=xmate, device_id_type=MESH
        ).wait_recv()

        for c in range(final):
            u = xh * final + c
            for h in range(2):
                low = c * CW + h * HW
                out[:, low : low + HW] = u_f32[u, h] + f32(r3[u, h])

        ref = u_b16.at[pl.ds((1 - xh) * final, final)]
        pltpu.make_async_remote_copy(
            ref, ref, x_send.at[0], x_recv.at[0], device_id=xmate, device_id_type=MESH
        ).wait_send()

    def leave(src, sem):
        pltpu.make_async_remote_copy(
            src, src, sem, a_recv.at[0, 0], device_id=mate, device_id_type=MESH
        ).wait_send()

    stages = ((0, product), (2, relay_one), (4, finish_one), (6, relay_two), (8, finish_two))
    n_rounds = final + FINALS

    @pl.loop(0, n_rounds + 8)
    def _(i):
        @pl.when(i == per_half)
        def _():
            gather(1)

        for lag, stage in stages:

            @pl.when((i >= lag) & (i < (final if lag == 0 else n_rounds + lag)))
            def _():
                for color in range(2):
                    stage(i - lag, color)

            if lag == 0:

                @pl.when((i >= final) & (i < n_rounds))
                def _():
                    for color in range(2):
                        product_final(i, color)

                @pl.when(i == 0)
                def _():
                    multiply(1, 2)
                    sum_cores(1, 1)
                    send_edges(1)

                @pl.when(i == 1)
                def _():
                    sum_cores(1, 2)

                @pl.when(i == per_half - 4)
                def _():
                    whiten(1)

                @pl.when(i == per_half - 2)
                def _():
                    pass_on(1)

                started = i - (per_half - 4) - (1 - xh) * 4

                @pl.when((started >= 0) & (started < 2 * FINALS))
                def _():
                    exchange(started)

    collect()

    leave(acc.at[:, :, :, 1 - core], a_send.at[0])
    leave(rxx.at[:, 1], a_send.at[1])
    leave(adj.at[:, 0:3], a_send.at[2])

    @pl.when(wide > 0)
    def _():
        leave(halo.at[:, 0], a_send.at[3])

    @pl.when(wide < 31)
    def _():
        leave(halo.at[:, 1], a_send.at[4])

    leave(s_buf.at[:, 0], b_send.at[0])
    leave(f1, b_send.at[1])
    leave(t_b16.at[:, 0], b_send.at[2])
    leave(f2, b_send.at[3])
    leave(x_out, x_send.at[1])


def shards(jacobian, prior_scale, lag_one, lag_two, noise_scale, sketch_seed):
    rows, width = jacobian.shape
    n = width // CW
    units = 2 * (n - FINALS)
    bf16, f32 = jnp.bfloat16, jnp.float32
    vmem = pl.BlockSpec(memory_space=pltpu.VMEM)
    product = pl.pallas_call(
        kernel,
        out_shape=jax.ShapeDtypeStruct((K // 32, width), f32),
        in_specs=[
            pl.BlockSpec(memory_space=pl.ANY), vmem, vmem, vmem, vmem,
            pl.BlockSpec(memory_space=pltpu.SMEM),
        ],
        out_specs=vmem,
        scratch_shapes=[
            pltpu.VMEM((rows, width), bf16),
            pltpu.VMEM((KH, width), bf16),
            pltpu.VMEM((2, 4, 2, 2, Q, BLOCK), f32),
            pltpu.VMEM((2, 4, 2, Q, BLOCK), f32),
            pltpu.VMEM((2, 2, 4, Q, BLOCK), f32),
            pltpu.VMEM((2, Q, rows + 256), f32),
            pltpu.VMEM((2, 2, Q, 128), f32),
            pltpu.VMEM((2, 4, Q, rows), bf16),
            pltpu.VMEM((units, 2, 4, 4, 16, HW), bf16),
            pltpu.VMEM((units, 2, 4, 16, HW), bf16),
            pltpu.VMEM((units, 4, 4, 16, HW), bf16),
            pltpu.VMEM((units, 2, 4, 16, HW), bf16),
            pltpu.VMEM((units, 2, 4, 16, HW), f32),
            pltpu.VMEM((units, 2, 4, 16, HW), bf16),
            pltpu.VMEM((units, 2, 16, HW), bf16),
            pltpu.VMEM((units, 4, 16, HW), bf16),
            pltpu.VMEM((units, 2, 16, HW), bf16),
            pltpu.VMEM((units, 2, 16, HW), f32),
            pltpu.VMEM((units, 2, 16, HW), bf16),
            pltpu.VMEM((units, 2, 16, HW), bf16),
            pltpu.VMEM((2 * FINALS, 2, 4, 4, 16, HW), bf16),
            pltpu.VMEM((2 * FINALS, 2, 4, 4, 16, HW), bf16),
            pltpu.SemaphoreType.DMA((4,)),
            pltpu.SemaphoreType.DMA((5,)),
            pltpu.SemaphoreType.DMA((2, 13)),
            pltpu.SemaphoreType.DMA((4,)),
            pltpu.SemaphoreType.DMA((2 * SLOTS, 4)),
            pltpu.SemaphoreType.DMA((2,)),
            pltpu.SemaphoreType.DMA((1 + 2 * FINALS,)),
        ],
        compiler_params=pltpu.CompilerParams(
            collective_id=0, has_side_effects=True, vmem_limit_bytes=63 * 1024 * 1024
        ),
    )(
        jacobian, prior_scale.reshape(1, width), lag_one.reshape(1, S), lag_two.reshape(1, S),
        noise_scale.reshape(1, S), sketch_seed,
    )
    return product * prior_scale[None, :]


def solution(mesh):
    in_specs = (P("wide", "narrow"), P("narrow"), P(), P(), P(), P())
    out_specs = P("wide", "narrow")
    return jax.shard_map(shards, mesh=mesh, in_specs=in_specs, out_specs=out_specs, check_vma=False)
```
